32 devices in a mesh: parts: 2 (over y), section: 2 (over core), tp: 8 (over z, x).
Axes of the slice: x: 2, y: 2, z: 4, core: 2. Of those that a mesh axis runs over, the one named last changes fastest.
Arguments:
- prompt_rows: bfloat16 [128, 8192], P(('parts', 'section', 'tp')), parts along dimension 0, may hold values from -72 to 72
- query_weight: bfloat16 [8192, 8192], P(None, 'tp'), may hold values from -0.0625 to 0.0625
- cache_weight: bfloat16 [8, 8192, 256], P('tp'), may hold values from -1 to 1, as said below
- output_weight: bfloat16 [8192, 8192], P('tp'), may hold values from -0.0625 to 0.0625
- documents: int32 [128], P('parts'), parts along dimension 0, may hold values from 0 to 3, never falling along the last dimension, each value on 1 to 32 neighbouring positions
- page_table: int32 [24], P('parts'), parts along dimension 0, may hold values from 0 to 15, as said below
Outputs:
- branch_output: bfloat16 [128, 8192], P(('parts', 'section', 'tp')), parts along dimension 0
- page_pool: bfloat16 [32, 8, 2048], P(('parts', 'section', 'tp')), parts along dimension 0
The draws below stay inside these ranges and needn't reach their ends.
There are 2 independent parts, one for each index of `parts`. The reference program is written for one: setup_inputs(seed, part) draws one part's arguments, and reference() takes and returns one part's arrays. A program takes and returns all parts, laid end to end along the dimension named above; an argument that names none is the same for every part. Nothing has to cross between parts.
Inputs may be any that keep to these rules, and one draw needn't show every extreme that they name: `cache_weight`: entry t equals entry u whenever t == u. `documents`: ids never fall along the tokens; there are 4 prompts of 1 to 32 tokens, one of exactly 32. `page_table`: entries are distinct pool slots; slot q is owned by the device of index q along section+tp (one slot per device). Entries beyond the number of pages are not used.
All inputs are finite; a program needn't handle non-finite values.
Results may differ from the reference program's by a relative error of at most 0.0085.
The reference program's roundings to bfloat16 on the way (of `queries`, `weights` and `attention`) count: a program that leaves them out, or rounds other values in their place, can miss the bound.
Values may be sent and summed in bfloat16 or wider, within the bound.
A program may use at most 64 MiB of HBM per device.

```python
import math
import jax
import jax.numpy as jnp
import numpy as np
from jax import lax

D = 8192
HEADS = 64
KV_HEADS = 8
HEAD = 128
PAGE = 8
TOKENS = 64
DOCS = 4
LONGEST = 32
MAXP = 12
POOL = 16
N_TP = 8


def draw_prompt_rows(key, part):
    first_key = jax.random.fold_in(key, 11)
    values = jnp.clip(jax.random.normal(first_key, (TOKENS, D), jnp.float32), -6.0, 6.0)
    return values.astype(jnp.bfloat16)


def draw_cache_weight(key, part):
    base_key = jax.random.fold_in(key, 21)
    base = jnp.clip(jax.random.normal(base_key, (KV_HEADS, D, 2 * HEAD), jnp.float32), -6.0, 6.0)
    base = (base / jnp.sqrt(jnp.float32(D))).astype(jnp.bfloat16)
    return jnp.repeat(base, N_TP // KV_HEADS, axis=0)


def draw_page_table(key, part):
    table_key = jax.random.fold_in(key, 31)
    return jax.random.permutation(table_key, POOL)[:MAXP].astype(jnp.int32)


def level_of(stream_key, dims, cuts, smallest, high):
    def one(axis_at, parts):
        heights = jax.random.uniform(jax.random.fold_in(jax.random.fold_in(stream_key, 6), axis_at), (parts,), jnp.float32, smallest / len(cuts), high / len(cuts))
        return jnp.repeat(jnp.exp(heights), dims[axis_at] // parts).reshape((-1,) + (1,) * (len(dims) - axis_at - 1))

    level = one(*cuts[0])
    for cut in cuts[1:]:
        level = level * one(*cut)
    return level


def split_up(amount, total, most, skew):
    weights = [(1 << 20) // math.isqrt(rank ** skew) + 1 for rank in range(2, amount + 1)]
    surplus, holding = total - most - (amount - 1), [1] * (amount - 1)
    while surplus > 0:
        free = [i for i in range(amount - 1) if holding[i] < most]
        whole, budget = sum([weights[i] for i in free]), surplus
        for i in free:
            more = min(most - holding[i], max(1, budget * weights[i] // whole), surplus)
            holding[i] = holding[i] + more
            surplus = surplus - more
    return np.array([most] + holding)


def uneven_parts(key, amount, total, most, slope):
    if amount == 2:
        one = jax.random.randint(key, (), max(1, total - most), min(most, total - 1) + 1)
        return jnp.stack([one, total - one])
    tallies = jnp.asarray(split_up(amount, total, most, slope), jnp.int32)
    pairs = (amount - 1) // 2
    donor, taker = tallies[1:1 + 2 * pairs:2], tallies[2:2 + 2 * pairs:2]
    margin = jnp.minimum(donor - 1, most - taker)
    shifted = jax.random.randint(jax.random.fold_in(key, 1), (pairs,), 0, 1 << 20) % (margin + 1)
    tallies = tallies.at[1:1 + 2 * pairs:2].set(donor - shifted).at[2:2 + 2 * pairs:2].set(taker + shifted)
    return tallies[jax.random.permutation(jax.random.fold_in(key, 2), amount)]


def centred(stream_key, extent, scale, bound, pieces=(), kind=jnp.bfloat16):
    array = jax.random.normal(stream_key, extent, jnp.float32) * scale
    if len(pieces) > 0:
        array = level_of(stream_key, extent, pieces, -0.22, 0.18) * array
    return jnp.clip(array, min=-bound, max=bound).astype(kind)


def setup_inputs(seed: int = 0, part: int = 0) -> dict:
    seeds = jax.random.split(jax.random.key(seed), 7)
    own_keys = jax.random.split(jax.random.fold_in(seeds[6], part), 7)
    return {
        "prompt_rows": draw_prompt_rows(jax.random.fold_in(jax.random.fold_in(seeds[6], part), 71), part),
        "query_weight": centred(seeds[1], (D, HEADS * HEAD), D ** -0.5, 0.0625, ((1, 8),)),
        "cache_weight": draw_cache_weight(jax.random.fold_in(seeds[6], 71), part),
        "output_weight": centred(seeds[3], (HEADS * HEAD, D), (HEADS * HEAD) ** -0.5, 0.0625, ((0, 8),)),
        "documents": jnp.searchsorted(jnp.cumsum(uneven_parts(own_keys[4], DOCS, TOKENS, LONGEST, 2)), jnp.arange(TOKENS), side="right").astype(jnp.int32),
        "page_table": draw_page_table(jax.random.fold_in(jax.random.fold_in(seeds[6], part), 71), part),
    }


rope_base = 500000.0


def document_layout(documents):
    count = documents.shape[0]
    places = jnp.arange(count, dtype=jnp.int32)
    begins = jnp.concatenate([jnp.ones((1,), dtype=bool), documents[1:] != documents[:-1]])
    firsts = lax.cummax(jnp.where(begins, places, jnp.zeros_like(places)), axis=0)
    offsets = (places - firsts).astype(jnp.int32)
    starts = (offsets % PAGE == 0).astype(jnp.int32)
    pages = (jnp.cumsum(starts) - 1).astype(jnp.int32)
    return offsets, pages


def rope_tables(offsets, width):
    half_width = width // 2
    freqs = rope_base ** (-(jnp.arange(half_width, dtype=jnp.float32) * 2.0 / width))
    angles = offsets.astype(jnp.float32)[:, None] * freqs[None, :]
    return jnp.cos(angles), jnp.sin(angles)


def rotate(values, cosines, sines):
    half_width = values.shape[-1] // 2
    first = values[..., :half_width]
    second = values[..., half_width:]
    return jnp.concatenate([first * cosines - second * sines, second * cosines + first * sines], axis=-1)


def reference(prompt_rows, query_weight, cache_weight, output_weight, documents, page_table):
    offsets, pages = document_layout(documents)
    cosines, sines = rope_tables(offsets, HEAD)
    queries = jnp.dot(prompt_rows, query_weight, preferred_element_type=jnp.float32)
    queries = queries.reshape(TOKENS, HEADS, HEAD)
    queries = rotate(queries, cosines[:, None, :], sines[:, None, :]).astype(jnp.bfloat16)
    copies = N_TP // KV_HEADS
    heads_weight = cache_weight[::copies]
    flat_weight = jnp.transpose(heads_weight, (1, 0, 2)).reshape(D, KV_HEADS * 2 * HEAD)
    keyvals = jnp.dot(prompt_rows, flat_weight, preferred_element_type=jnp.float32)
    keyvals = keyvals.reshape(TOKENS, KV_HEADS, 2 * HEAD)
    keys = rotate(keyvals[..., :HEAD], cosines[:, None, :], sines[:, None, :]).astype(jnp.bfloat16)
    values = keyvals[..., HEAD:].astype(jnp.bfloat16)
    places = jnp.arange(TOKENS, dtype=jnp.int32)
    allowed = (documents[:, None] == documents[None, :]) & (places[None, :] <= places[:, None])
    scale = 1.0 / (HEAD ** 0.5)
    group_size = HEADS // KV_HEADS

    def one_head(index):
        query = lax.dynamic_index_in_dim(queries, index, 1, keepdims=False)
        group = index // group_size
        key = lax.dynamic_index_in_dim(keys, group, 1, keepdims=False)
        value = lax.dynamic_index_in_dim(values, group, 1, keepdims=False)
        scores = jnp.dot(query, key.T, preferred_element_type=jnp.float32) * scale
        scores = jnp.where(allowed, scores, -jnp.inf)
        weights = jax.nn.softmax(scores, axis=-1).astype(jnp.bfloat16)
        return jnp.dot(weights, value, preferred_element_type=jnp.float32).astype(jnp.bfloat16)

    heads_out = lax.map(one_head, jnp.arange(HEADS, dtype=jnp.int32))
    attention = jnp.transpose(heads_out, (1, 0, 2)).reshape(TOKENS, HEADS * HEAD)
    branch_output = jnp.dot(attention, output_weight, preferred_element_type=jnp.float32).astype(jnp.bfloat16)
    cache_rows = jnp.concatenate([keys.reshape(TOKENS, KV_HEADS * HEAD), values.reshape(TOKENS, KV_HEADS * HEAD)], axis=1)
    row_of = (page_table[pages] * PAGE + offsets % PAGE).astype(jnp.int32)
    pool = jnp.zeros((POOL * PAGE, 2 * KV_HEADS * HEAD), jnp.bfloat16).at[row_of].set(cache_rows)
    return branch_output, pool.reshape(POOL, PAGE, 2 * KV_HEADS * HEAD)
```

```python
import functools
import math

import jax
import jax.numpy as jnp
from jax import lax
from jax.experimental import pallas as pl
from jax.experimental.pallas import tpu as pltpu
from jax.sharding import PartitionSpec as P

KV_HEADS = 8
HEAD = 128
PAGE = 8
K_CHUNKS = 4
N_CHUNKS = 4
MESH = pl.DeviceIdType.MESH


rope_base = 500000.0


def from_partner(value, axis, distance):
    mask = 2**distance
    pairs = [(source, source ^ mask) for source in range(lax.axis_size(axis))]
    return lax.ppermute(value, axis, pairs)


def document_layout(documents):
    count = documents.shape[0]
    places = jnp.arange(count, dtype=jnp.int32)
    begins = jnp.concatenate([jnp.ones((1,), dtype=bool), documents[1:] != documents[:-1]])
    firsts = lax.cummax(jnp.where(begins, places, jnp.zeros_like(places)), axis=0)
    offsets = places - firsts
    starts = (offsets % PAGE == 0).astype(jnp.int32)
    pages = jnp.cumsum(starts) - 1
    return (offsets, pages)


def rope_tables(offsets, width):
    half_width = width // 2
    freqs = rope_base ** (-(jnp.arange(half_width, dtype=jnp.float32) * 2.0 / width))
    angles = offsets.astype(jnp.float32)[:, None] * freqs[None, :]
    return (jnp.cos(angles), jnp.sin(angles))


def rotate(values, cosines, sines):
    half_width = values.shape[-1] // 2
    first = values[..., :half_width]
    second = values[..., half_width:]
    return jnp.concatenate(
        [first * cosines - second * sines, second * cosines + first * sines], axis=-1
    )


def finish_cache(keyvals, cosines, sines):
    rotated = rotate(keyvals[:, :HEAD], cosines, sines)
    return jnp.concatenate([rotated, keyvals[:, HEAD:]], axis=1).astype(jnp.bfloat16)


def body(prompt_rows, query_weight, cache_weight, output_weight, documents, page_table):
    tp_count = lax.axis_size("tp")
    owners = lax.axis_size(("section", "tp"))
    section = lax.axis_index("section")
    column = lax.axis_index("tp")
    rows_dev = prompt_rows.shape[0]
    half_rows = rows_dev * tp_count
    total_rows = 2 * half_rows
    query_width = query_weight.shape[1]
    query_heads = query_width // HEAD
    replicas = tp_count // KV_HEADS
    slice_width = HEAD // replicas
    head_weight = cache_weight[0]
    offsets, pages = document_layout(documents)
    cosines, sines = rope_tables(offsets, HEAD)
    own_start = section * half_rows
    own_cos = lax.dynamic_slice_in_dim(cosines, own_start, half_rows, 0)
    own_sin = lax.dynamic_slice_in_dim(sines, own_start, half_rows, 0)
    piece = lax.all_gather(prompt_rows, "tp", axis=0, tiled=True)
    query_rows = jnp.dot(piece, query_weight, preferred_element_type=jnp.float32)
    cache_rows = jnp.dot(piece, head_weight, preferred_element_type=jnp.float32)
    joined = jnp.concatenate([query_rows, cache_rows], axis=1)
    query_part = joined[:, :query_width]
    cache_half = finish_cache(joined[:, query_width:], own_cos, own_sin)
    other = from_partner(cache_half, "section", 0)
    lower = jnp.where(section == 0, cache_half, other)
    upper = jnp.where(section == 0, other, cache_half)
    cache_all = jnp.concatenate([lower, upper], axis=0)
    queries = query_part.reshape(half_rows, query_heads, HEAD)
    queries = rotate(queries, own_cos[:, None, :], own_sin[:, None, :]).astype(jnp.bfloat16)
    keys = cache_all[:, :HEAD]
    values = cache_all[:, HEAD:]
    places = jnp.arange(total_rows, dtype=jnp.int32)
    query_places = own_start + jnp.arange(half_rows, dtype=jnp.int32)
    query_docs = lax.dynamic_slice_in_dim(documents, own_start, half_rows, 0)
    allowed = (query_docs[:, None] == documents[None, :]) & (
        places[None, :] <= query_places[:, None]
    )
    scale = 1.0 / HEAD**0.5
    scores = jnp.einsum("qhd,kd->hqk", queries, keys, preferred_element_type=jnp.float32) * scale
    scores = jnp.where(allowed[None, :, :], scores, -jnp.inf)
    weights = jax.nn.softmax(scores, axis=-1).astype(jnp.bfloat16)
    mixed = jnp.einsum("hqk,kd->qhd", weights, values, preferred_element_type=jnp.float32)
    attention = mixed.astype(jnp.bfloat16).reshape(half_rows, query_heads * HEAD)
    summed = lax.psum_scatter(
        jnp.dot(attention, output_weight, preferred_element_type=jnp.float32),
        "tp",
        scatter_dimension=0,
        tiled=True,
    )
    branch_output = summed.astype(jnp.bfloat16)
    column_start = section * HEAD + column % replicas * slice_width
    share = lax.dynamic_slice_in_dim(cache_all, column_start, slice_width, 1)
    capacity = rows_dev // 4 * PAGE
    row_of = page_table[pages] * PAGE + offsets % PAGE
    outgoing = jnp.zeros((owners * capacity, slice_width), jnp.bfloat16).at[row_of].set(share)
    outgoing = outgoing.reshape(owners, capacity, slice_width)
    arrived = lax.all_to_all(outgoing, ("section", "tp"), split_axis=0, concat_axis=2, tiled=True)
    return (branch_output, arrived)


def fused_kernel(
    sizes,
    rows_hbm,
    wq_hbm,
    wkv_hbm,
    wo_hbm,
    docs_ref,
    table_ref,
    out_ref,
    pool_ref,
    xbuf,
    wq,
    wkv,
    wo,
    acc_q,
    acc_kv,
    kv_all,
    pagebuf,
    pagerecv,
    attn,
    sendbuf,
    recvbuf,
    x_send,
    x_recv,
    x_local,
    w_sem,
    wo_sem,
    kv_send,
    kv_recv,
    page_send,
    page_recv,
    page_local,
    r_send,
    r_recv,
):
    tp_count, section_count, k_chunks, n_chunks = sizes
    part = lax.axis_index("parts")
    section = lax.axis_index("section")
    me = lax.axis_index("tp")
    rows_dev, depth = rows_hbm.shape
    half_rows = rows_dev * tp_count
    total_rows = section_count * half_rows
    kc = depth // k_chunks
    width = wq_hbm.shape[1]
    heads = width // HEAD
    out_width = wo_hbm.shape[1]
    nc = out_width // n_chunks
    owners = section_count * tp_count

    def peer(distance):
        return lax.rem(me + distance, tp_count)

    def device(sec, col):
        return (part, sec, col)

    barrier = pltpu.get_barrier_semaphore()
    for sec in range(section_count):
        for distance in range(tp_count):
            if sec == 0 and distance == 0:
                continue
            target = device(lax.rem(section + sec, section_count), peer(distance))
            pl.semaphore_signal(barrier, inc=1, device_id=target, device_id_type=MESH)

    def weight_copies(c):
        where = pl.ds(c * kc, kc)
        return (
            pltpu.make_async_copy(wkv_hbm.at[0, where], wkv.at[c], w_sem.at[c, 0]),
            pltpu.make_async_copy(wq_hbm.at[where], wq.at[c], w_sem.at[c, 1]),
        )

    def out_copy(n):
        return pltpu.make_async_copy(
            wo_hbm.at[:, pl.ds(pl.multiple_of(n * nc, nc), nc)], wo.at[n], wo_sem.at[n]
        )

    def row_copy(c, distance):
        return pltpu.make_async_remote_copy(
            src_ref=rows_hbm.at[:, pl.ds(pl.multiple_of(c * kc, kc), kc)],
            dst_ref=xbuf.at[c, me],
            send_sem=x_send.at[c, distance],
            recv_sem=x_recv.at[c, distance],
            device_id=device(section, peer(distance)),
            device_id_type=MESH,
        )

    def own_rows(c):
        return pltpu.make_async_copy(
            rows_hbm.at[:, pl.ds(pl.multiple_of(c * kc, kc), kc)], xbuf.at[c, me], x_local.at[c]
        )

    for copy in weight_copies(0):
        copy.start()
    for c in range(k_chunks):
        own_rows(c).start()
    pl.semaphore_wait(barrier, owners - 1)
    for c in range(k_chunks):
        for distance in range(1, tp_count):
            row_copy(c, distance).start()
    for c in range(1, k_chunks):
        for copy in weight_copies(c):
            copy.start()
    for n in range(n_chunks):
        out_copy(n).start()

    docs = docs_ref[...].astype(jnp.float32)
    table = table_ref[...].astype(jnp.float32)

    def iota(shape, axis):
        return lax.broadcasted_iota(jnp.int32, shape, axis)

    def layout(count, start):
        row_at = iota((count, total_rows), 0) + start
        col_at = iota((count, total_rows), 1)
        own = jnp.sum(jnp.where(row_at == col_at, docs, 0.0), axis=1, keepdims=True)
        return row_at, col_at, own == docs

    def mod_page(values):
        return values - PAGE * jnp.floor(values * (1.0 / PAGE))

    row_at, col_at, same = layout(half_rows, section * half_rows)
    allowed = same & (col_at <= row_at)
    offset_own = jnp.sum(jnp.where(same & (col_at < row_at), 1.0, 0.0), axis=1, keepdims=True)
    lane = iota((half_rows, HEAD), 1)
    half = HEAD // 2
    second = lane >= half
    freq_at = jnp.where(second, lane - half, lane).astype(jnp.float32)
    freqs = jnp.exp(freq_at * (-2.0 / HEAD * math.log(rope_base)))
    angles = offset_own * freqs
    cosines = jnp.cos(angles)
    sines = jnp.sin(angles)
    sines = jnp.where(second, sines, -sines)

    row_at, col_at, same = layout(total_rows, 0)
    offset_col = jnp.sum(jnp.where(same & (col_at < row_at), 1.0, 0.0), axis=1, keepdims=True)
    offset_row = jnp.sum(jnp.where(same & (row_at < col_at), 1.0, 0.0), axis=0, keepdims=True)
    begins = jnp.where((mod_page(offset_col) == 0.0) & (row_at <= col_at), 1.0, 0.0)
    page_row = jnp.sum(begins, axis=0, keepdims=True) - 1.0
    slot_row = jnp.zeros_like(page_row)
    for p in range(table_ref.shape[1]):
        slot_row += jnp.where(page_row == float(p), table[:, p : p + 1], 0.0)
    place_row = slot_row * PAGE + mod_page(offset_row)
    place_at = iota((owners * PAGE, total_rows), 0).astype(jnp.float32)
    select = jnp.where(place_at == place_row, 1.0, 0.0).astype(jnp.bfloat16)

    def rotate_rows(values):
        return values * cosines + pltpu.roll(values, half, 1) * sines

    acc_q[...] = jnp.zeros_like(acc_q)
    acc_kv[...] = jnp.zeros_like(acc_kv)

    def project(c, carry):
        own_rows(c).wait()
        for distance in range(1, tp_count):
            row_copy(c, distance).wait_recv()
        pieces = [xbuf[c, t].astype(jnp.float32) for t in range(tp_count)]
        block = jnp.concatenate(pieces, axis=0).astype(jnp.bfloat16)
        copies = weight_copies(c)
        copies[0].wait()
        acc_kv[...] += jnp.dot(block, wkv[c], preferred_element_type=jnp.float32)
        copies[1].wait()
        acc_q[...] += jnp.dot(block, wq[c], preferred_element_type=jnp.float32)
        return carry

    lax.fori_loop(0, k_chunks, project, 0)

    keys_own = rotate_rows(acc_kv[:, :HEAD])
    kv_all[section] = jnp.concatenate([keys_own, acc_kv[:, HEAD:]], axis=1).astype(jnp.bfloat16)
    kv_copy = pltpu.make_async_remote_copy(
        src_ref=kv_all.at[section],
        dst_ref=kv_all.at[section],
        send_sem=kv_send,
        recv_sem=kv_recv,
        device_id=device(1 - section, me),
        device_id_type=MESH,
    )
    kv_copy.start()
    queries = jnp.concatenate(
        [rotate_rows(acc_q[:, h * HEAD : (h + 1) * HEAD]) for h in range(heads)], axis=0
    ).astype(jnp.bfloat16)
    kv_copy.wait()
    both = jnp.concatenate([kv_all[0], kv_all[1]], axis=0)

    paged = jnp.dot(select, both, preferred_element_type=jnp.float32).astype(jnp.bfloat16)
    for kind in range(2):
        for q in range(owners):
            pagebuf[kind, q] = paged[q * PAGE : (q + 1) * PAGE, kind * HEAD : (kind + 1) * HEAD]
    own_slot = section * tp_count + me

    def page_copy(sec, distance):
        sec_to = lax.rem(section + sec, section_count)
        to = peer(distance)
        return pltpu.make_async_remote_copy(
            src_ref=pagebuf.at[section, sec_to * tp_count + to],
            dst_ref=pagerecv.at[own_slot],
            send_sem=page_send.at[sec, distance],
            recv_sem=page_recv.at[sec, distance],
            device_id=device(sec_to, to),
            device_id_type=MESH,
        )

    others = [
        (sec, distance)
        for sec in range(section_count)
        for distance in range(tp_count)
        if sec or distance
    ]
    for sec, distance in others:
        page_copy(sec, distance).start()
    own_page = pltpu.make_async_copy(
        pagebuf.at[section, own_slot], pagerecv.at[own_slot], page_local
    )
    own_page.start()

    keys = both[:, :HEAD]
    values = both[:, HEAD:]
    scores = lax.dot_general(
        queries, keys, (((1,), (1,)), ((), ())), preferred_element_type=jnp.float32
    ) * (1.0 / HEAD**0.5)
    keep = jnp.concatenate([jnp.where(allowed, 1.0, 0.0)] * heads, axis=0)
    scores = jnp.where(keep > 0.5, scores, -jnp.inf)
    top = jnp.max(scores, axis=1, keepdims=True)
    powers = jnp.exp(scores - top)
    weights = (powers / jnp.sum(powers, axis=1, keepdims=True)).astype(jnp.bfloat16)
    mixed = jnp.dot(weights, values, preferred_element_type=jnp.float32).astype(jnp.bfloat16)
    for h in range(heads):
        attn[:, h * HEAD : (h + 1) * HEAD] = mixed[h * half_rows : (h + 1) * half_rows]

    def sum_copy(n, distance):
        to = peer(distance)
        return pltpu.make_async_remote_copy(
            src_ref=sendbuf.at[n, to],
            dst_ref=recvbuf.at[n, me],
            send_sem=r_send.at[n, distance],
            recv_sem=r_recv.at[n, distance],
            device_id=device(section, to),
            device_id_type=MESH,
        )

    def produce(n, carry):
        out_copy(n).wait()
        partial = jnp.dot(attn[...], wo[n], preferred_element_type=jnp.float32)
        for t in range(tp_count):
            sendbuf[n, t] = partial[t * rows_dev : (t + 1) * rows_dev].astype(jnp.bfloat16)
        for distance in range(1, tp_count):
            sum_copy(n, distance).start()
        return carry

    lax.fori_loop(0, n_chunks, produce, 0)

    own_page.wait()
    for sec, distance in others:
        page_copy(sec, distance).wait()
    for slot in range(owners):
        pool_ref[0, :, slot * HEAD : (slot + 1) * HEAD] = pagerecv[slot]

    for n in range(n_chunks):
        total = sendbuf[n, me].astype(jnp.float32)
        for distance in range(1, tp_count):
            sum_copy(n, distance).wait_recv()
            source = lax.rem(me + tp_count - distance, tp_count)
            total += recvbuf[n, source].astype(jnp.float32)
        out_ref[:, n * nc : (n + 1) * nc] = total.astype(jnp.bfloat16)

    for c in range(k_chunks):
        for distance in range(1, tp_count):
            row_copy(c, distance).wait_send()
    for n in range(n_chunks):
        for distance in range(1, tp_count):
            sum_copy(n, distance).wait_send()


def fused_body(prompt_rows, query_weight, cache_weight, output_weight, documents, page_table):
    tp_count = lax.axis_size("tp")
    section_count = lax.axis_size("section")
    rows_dev, depth = prompt_rows.shape
    width = query_weight.shape[1]
    out_width = output_weight.shape[1]
    half_rows = rows_dev * tp_count
    owners = section_count * tp_count
    k_chunks = K_CHUNKS
    n_chunks = N_CHUNKS
    kc, nc = depth // k_chunks, out_width // n_chunks
    bf16, f32 = jnp.bfloat16, jnp.float32
    dma = pltpu.SemaphoreType.DMA
    anywhere = pl.BlockSpec(memory_space=pl.ANY)
    local = pl.BlockSpec(memory_space=pltpu.VMEM)
    return pl.pallas_call(
        functools.partial(fused_kernel, (tp_count, section_count, k_chunks, n_chunks)),
        out_shape=(
            jax.ShapeDtypeStruct((rows_dev, out_width), bf16),
            jax.ShapeDtypeStruct((1, PAGE, owners * HEAD), bf16),
        ),
        in_specs=[anywhere] * 4 + [local] * 2,
        out_specs=(local, local),
        scratch_shapes=[
            pltpu.VMEM((k_chunks, tp_count, rows_dev, kc), bf16),
            pltpu.VMEM((k_chunks, kc, width), bf16),
            pltpu.VMEM((k_chunks, kc, 2 * HEAD), bf16),
            pltpu.VMEM((n_chunks, width, nc), bf16),
            pltpu.VMEM((half_rows, width), f32),
            pltpu.VMEM((half_rows, 2 * HEAD), f32),
            pltpu.VMEM((section_count, half_rows, 2 * HEAD), bf16),
            pltpu.VMEM((2, owners, PAGE, HEAD), bf16),
            pltpu.VMEM((owners, PAGE, HEAD), bf16),
            pltpu.VMEM((half_rows, width), bf16),
            pltpu.VMEM((n_chunks, tp_count, rows_dev, nc), bf16),
            pltpu.VMEM((n_chunks, tp_count, rows_dev, nc), bf16),
            dma((k_chunks, tp_count)),
            dma((k_chunks, tp_count)),
            dma((k_chunks,)),
            dma((k_chunks, 2)),
            dma((n_chunks,)),
            dma,
            dma,
            dma((section_count, tp_count)),
            dma((section_count, tp_count)),
            dma,
            dma((n_chunks, tp_count)),
            dma((n_chunks, tp_count)),
        ],
        compiler_params=pltpu.CompilerParams(
            collective_id=0, has_side_effects=True, vmem_limit_bytes=60 * 1024 * 1024
        ),
    )(
        prompt_rows,
        query_weight,
        cache_weight,
        output_weight,
        documents.reshape(1, -1),
        page_table.reshape(1, -1),
    )


def fits(prompt_rows, query_weight, page_table):
    tp_count = lax.axis_size("tp")
    one_copy = tp_count == KV_HEADS
    one_slot = prompt_rows.shape[0] // 4 == 1
    return one_copy and one_slot and lax.axis_size("section") == 2


def choose(prompt_rows, query_weight, cache_weight, output_weight, documents, page_table):
    plan = fused_body if fits(prompt_rows, query_weight, page_table) else body
    return plan(prompt_rows, query_weight, cache_weight, output_weight, documents, page_table)


def solution(mesh):
    return jax.shard_map(
        choose,
        mesh=mesh,
        in_specs=(
            P(("parts", "section", "tp"), None),
            P(None, "tp"),
            P("tp", None, None),
            P("tp", None),
            P("parts"),
            P("parts"),
        ),
        out_specs=(P(("parts", "section", "tp"), None), P(("parts", "section", "tp"), None, None)),
        check_vma=False,
    )
```

```python
import functools
import math

import jax
import jax.numpy as jnp
from jax import lax
from jax.experimental import pallas as pl
from jax.experimental.pallas import tpu as pltpu
from jax.sharding import PartitionSpec as P

KV_HEADS = 8
HEAD = 128
PAGE = 8
K_CHUNKS = 2
N_CHUNKS = 2
MESH = pl.DeviceIdType.MESH
FAR = (4, 6)
NEAR = (1, 2, 3)
HANDED = (5, 7)


rope_base = 500000.0


def from_partner(value, axis, distance):
    mask = 2**distance
    pairs = [(source, source ^ mask) for source in range(lax.axis_size(axis))]
    return lax.ppermute(value, axis, pairs)


def document_layout(documents):
    count = documents.shape[0]
    places = jnp.arange(count, dtype=jnp.int32)
    begins = jnp.concatenate([jnp.ones((1,), dtype=bool), documents[1:] != documents[:-1]])
    firsts = lax.cummax(jnp.where(begins, places, jnp.zeros_like(places)), axis=0)
    offsets = places - firsts
    starts = (offsets % PAGE == 0).astype(jnp.int32)
    pages = jnp.cumsum(starts) - 1
    return (offsets, pages)


def rope_tables(offsets, width):
    half_width = width // 2
    freqs = rope_base ** (-(jnp.arange(half_width, dtype=jnp.float32) * 2.0 / width))
    angles = offsets.astype(jnp.float32)[:, None] * freqs[None, :]
    return (jnp.cos(angles), jnp.sin(angles))


def rotate(values, cosines, sines):
    half_width = values.shape[-1] // 2
    first = values[..., :half_width]
    second = values[..., half_width:]
    return jnp.concatenate(
        [first * cosines - second * sines, second * cosines + first * sines], axis=-1
    )


def finish_cache(keyvals, cosines, sines):
    rotated = rotate(keyvals[:, :HEAD], cosines, sines)
    return jnp.concatenate([rotated, keyvals[:, HEAD:]], axis=1).astype(jnp.bfloat16)


def body(prompt_rows, query_weight, cache_weight, output_weight, documents, page_table):
    tp_count = lax.axis_size("tp")
    owners = lax.axis_size(("section", "tp"))
    section = lax.axis_index("section")
    column = lax.axis_index("tp")
    rows_dev = prompt_rows.shape[0]
    half_rows = rows_dev * tp_count
    total_rows = 2 * half_rows
    query_width = query_weight.shape[1]
    query_heads = query_width // HEAD
    replicas = tp_count // KV_HEADS
    slice_width = HEAD // replicas
    head_weight = cache_weight[0]
    offsets, pages = document_layout(documents)
    cosines, sines = rope_tables(offsets, HEAD)
    own_start = section * half_rows
    own_cos = lax.dynamic_slice_in_dim(cosines, own_start, half_rows, 0)
    own_sin = lax.dynamic_slice_in_dim(sines, own_start, half_rows, 0)
    piece = lax.all_gather(prompt_rows, "tp", axis=0, tiled=True)
    query_rows = jnp.dot(piece, query_weight, preferred_element_type=jnp.float32)
    cache_rows = jnp.dot(piece, head_weight, preferred_element_type=jnp.float32)
    joined = jnp.concatenate([query_rows, cache_rows], axis=1)
    query_part = joined[:, :query_width]
    cache_half = finish_cache(joined[:, query_width:], own_cos, own_sin)
    other = from_partner(cache_half, "section", 0)
    lower = jnp.where(section == 0, cache_half, other)
    upper = jnp.where(section == 0, other, cache_half)
    cache_all = jnp.concatenate([lower, upper], axis=0)
    queries = query_part.reshape(half_rows, query_heads, HEAD)
    queries = rotate(queries, own_cos[:, None, :], own_sin[:, None, :]).astype(jnp.bfloat16)
    keys = cache_all[:, :HEAD]
    values = cache_all[:, HEAD:]
    places = jnp.arange(total_rows, dtype=jnp.int32)
    query_places = own_start + jnp.arange(half_rows, dtype=jnp.int32)
    query_docs = lax.dynamic_slice_in_dim(documents, own_start, half_rows, 0)
    allowed = (query_docs[:, None] == documents[None, :]) & (
        places[None, :] <= query_places[:, None]
    )
    scale = 1.0 / HEAD**0.5
    scores = jnp.einsum("qhd,kd->hqk", queries, keys, preferred_element_type=jnp.float32) * scale
    scores = jnp.where(allowed[None, :, :], scores, -jnp.inf)
    weights = jax.nn.softmax(scores, axis=-1).astype(jnp.bfloat16)
    mixed = jnp.einsum("hqk,kd->qhd", weights, values, preferred_element_type=jnp.float32)
    attention = mixed.astype(jnp.bfloat16).reshape(half_rows, query_heads * HEAD)
    summed = lax.psum_scatter(
        jnp.dot(attention, output_weight, preferred_element_type=jnp.float32),
        "tp",
        scatter_dimension=0,
        tiled=True,
    )
    branch_output = summed.astype(jnp.bfloat16)
    column_start = section * HEAD + column % replicas * slice_width
    share = lax.dynamic_slice_in_dim(cache_all, column_start, slice_width, 1)
    capacity = rows_dev // 4 * PAGE
    row_of = page_table[pages] * PAGE + offsets % PAGE
    outgoing = jnp.zeros((owners * capacity, slice_width), jnp.bfloat16).at[row_of].set(share)
    outgoing = outgoing.reshape(owners, capacity, slice_width)
    arrived = lax.all_to_all(outgoing, ("section", "tp"), split_axis=0, concat_axis=2, tiled=True)
    return (branch_output, arrived)


def fused_kernel(
    sizes,
    rows_hbm,
    wq_hbm,
    wkv_hbm,
    wo_hbm,
    docs_ref,
    table_ref,
    out_ref,
    pool_ref,
    xbuf,
    wq,
    wkv,
    wo,
    acc_q,
    acc_kv,
    kv_all,
    pagebuf,
    pagerecv,
    attn,
    sendbuf,
    recvbuf,
    held,
    joined,
    x_send,
    x_recv,
    x_local,
    w_sem,
    wo_sem,
    kv_send,
    kv_recv,
    page_send,
    page_recv,
    page_local,
    r_send,
    r_recv,
):
    tp_count, section_count, k_chunks, n_chunks = sizes
    part = lax.axis_index("parts")
    section = lax.axis_index("section")
    me = lax.axis_index("tp")
    rows_dev, depth = rows_hbm.shape
    half_rows = rows_dev * tp_count
    total_rows = section_count * half_rows
    kc = depth // k_chunks
    width = wq_hbm.shape[1]
    heads = width // HEAD
    out_width = wo_hbm.shape[1]
    nc = out_width // n_chunks
    owners = section_count * tp_count

    def peer(distance):
        return lax.rem(me + distance, tp_count)

    def mate(mask):
        index = 0
        for bit in (1, 2, 4):
            digit = lax.rem(lax.div(me, bit), 2)
            index = index + bit * (1 - digit if mask & bit else digit)
        return index

    def device(sec, col):
        return (part, sec, col)

    barrier = pltpu.get_barrier_semaphore()
    for sec in range(section_count):
        for distance in range(tp_count):
            if sec == 0 and distance == 0:
                continue
            target = device(lax.rem(section + sec, section_count), peer(distance))
            pl.semaphore_signal(barrier, inc=1, device_id=target, device_id_type=MESH)

    def weight_copies(c):
        where = pl.ds(c * kc, kc)
        return (
            pltpu.make_async_copy(wkv_hbm.at[0, where], wkv.at[c], w_sem.at[c, 0]),
            pltpu.make_async_copy(wq_hbm.at[where], wq.at[c], w_sem.at[c, 1]),
        )

    def out_copy(n):
        return pltpu.make_async_copy(
            wo_hbm.at[:, pl.ds(pl.multiple_of(n * nc, nc), nc)], wo.at[n], wo_sem.at[n]
        )

    def row_copy(c, mask):
        return pltpu.make_async_remote_copy(
            src_ref=rows_hbm.at[:, pl.ds(pl.multiple_of(c * kc, kc), kc)],
            dst_ref=xbuf.at[c, me],
            send_sem=x_send.at[c, mask],
            recv_sem=x_recv.at[c, mask],
            device_id=device(section, mate(mask)),
            device_id_type=MESH,
        )

    def pass_on(c, mask):
        return pltpu.make_async_remote_copy(
            src_ref=xbuf.at[c, mate(mask)],
            dst_ref=xbuf.at[c, mate(mask)],
            send_sem=x_send.at[c, mask ^ 1],
            recv_sem=x_recv.at[c, mask ^ 1],
            device_id=device(section, mate(1)),
            device_id_type=MESH,
        )

    def forward(c):
        for mask in FAR:
            row_copy(c, mask).wait_recv()
            pass_on(c, mask).start()

    def own_rows(c):
        return pltpu.make_async_copy(
            rows_hbm.at[:, pl.ds(pl.multiple_of(c * kc, kc), kc)], xbuf.at[c, me], x_local.at[c]
        )

    for copy in weight_copies(0):
        copy.start()
    for c in range(k_chunks):
        own_rows(c).start()
    pl.semaphore_wait(barrier, owners - 1)
    for c in range(k_chunks):
        for mask in FAR + NEAR:
            row_copy(c, mask).start()
    for c in range(1, k_chunks):
        for copy in weight_copies(c):
            copy.start()
    for n in range(n_chunks):
        out_copy(n).start()

    docs = docs_ref[...].astype(jnp.float32)
    table = table_ref[...].astype(jnp.float32)

    def iota(shape, axis):
        return lax.broadcasted_iota(jnp.int32, shape, axis)

    def layout(count, start):
        row_at = iota((count, total_rows), 0) + start
        col_at = iota((count, total_rows), 1)
        own = jnp.sum(jnp.where(row_at == col_at, docs, 0.0), axis=1, keepdims=True)
        return row_at, col_at, own == docs

    def mod_page(values):
        return values - PAGE * jnp.floor(values * (1.0 / PAGE))

    row_at, col_at, same = layout(half_rows, section * half_rows)
    allowed = same & (col_at <= row_at)
    offset_own = jnp.sum(jnp.where(same & (col_at < row_at), 1.0, 0.0), axis=1, keepdims=True)
    lane = iota((half_rows, HEAD), 1)
    half = HEAD // 2
    second = lane >= half
    freq_at = jnp.where(second, lane - half, lane).astype(jnp.float32)
    freqs = jnp.exp(freq_at * (-2.0 / HEAD * math.log(rope_base)))
    angles = offset_own * freqs
    cosines = jnp.cos(angles)
    sines = jnp.sin(angles)
    sines = jnp.where(second, sines, -sines)

    row_at, col_at, same = layout(total_rows, 0)
    offset_col = jnp.sum(jnp.where(same & (col_at < row_at), 1.0, 0.0), axis=1, keepdims=True)
    offset_row = jnp.sum(jnp.where(same & (row_at < col_at), 1.0, 0.0), axis=0, keepdims=True)
    begins = jnp.where((mod_page(offset_col) == 0.0) & (row_at <= col_at), 1.0, 0.0)
    page_row = jnp.sum(begins, axis=0, keepdims=True) - 1.0
    slot_row = jnp.zeros_like(page_row)
    for p in range(table_ref.shape[1]):
        slot_row += jnp.where(page_row == float(p), table[:, p : p + 1], 0.0)
    place_row = slot_row * PAGE + mod_page(offset_row)
    place_at = iota((owners * PAGE, total_rows), 0).astype(jnp.float32)
    select = jnp.where(place_at == place_row, 1.0, 0.0).astype(jnp.bfloat16)

    def rotate_rows(values):
        return values * cosines + pltpu.roll(values, half, 1) * sines

    acc_q[...] = jnp.zeros_like(acc_q)
    acc_kv[...] = jnp.zeros_like(acc_kv)

    forward(0)

    def project(c, carry):
        @pl.when(c + 1 < k_chunks)
        def _():
            forward(c + 1)

        own_rows(c).wait()
        for mask in NEAR:
            row_copy(c, mask).wait_recv()
        for mask in FAR:
            pass_on(c, mask).wait_recv()
        pieces = [xbuf[c, t].astype(jnp.float32) for t in range(tp_count)]
        block = jnp.concatenate(pieces, axis=0).astype(jnp.bfloat16)
        copies = weight_copies(c)
        copies[0].wait()
        acc_kv[...] += jnp.dot(block, wkv[c], preferred_element_type=jnp.float32)
        copies[1].wait()
        acc_q[...] += jnp.dot(block, wq[c], preferred_element_type=jnp.float32)
        return carry

    lax.fori_loop(0, k_chunks, project, 0)

    keys_own = rotate_rows(acc_kv[:, :HEAD])
    kv_all[section] = jnp.concatenate([keys_own, acc_kv[:, HEAD:]], axis=1).astype(jnp.bfloat16)
    kv_copy = pltpu.make_async_remote_copy(
        src_ref=kv_all.at[section],
        dst_ref=kv_all.at[section],
        send_sem=kv_send,
        recv_sem=kv_recv,
        device_id=device(1 - section, me),
        device_id_type=MESH,
    )
    kv_copy.start()
    queries = jnp.concatenate(
        [rotate_rows(acc_q[:, h * HEAD : (h + 1) * HEAD]) for h in range(heads)], axis=0
    ).astype(jnp.bfloat16)
    kv_copy.wait()
    both = jnp.concatenate([kv_all[0], kv_all[1]], axis=0)

    paged = jnp.dot(select, both, preferred_element_type=jnp.float32).astype(jnp.bfloat16)
    for kind in range(2):
        for q in range(owners):
            pagebuf[kind, q] = paged[q * PAGE : (q + 1) * PAGE, kind * HEAD : (kind + 1) * HEAD]
    own_slot = section * tp_count + me

    def page_copy(sec, distance):
        sec_to = lax.rem(section + sec, section_count)
        to = peer(distance)
        return pltpu.make_async_remote_copy(
            src_ref=pagebuf.at[section, sec_to * tp_count + to],
            dst_ref=pagerecv.at[own_slot],
            send_sem=page_send.at[sec, distance],
            recv_sem=page_recv.at[sec, distance],
            device_id=device(sec_to, to),
            device_id_type=MESH,
        )

    others = [
        (sec, distance)
        for sec in range(section_count)
        for distance in range(tp_count)
        if sec or distance
    ]
    for sec, distance in others:
        page_copy(sec, distance).start()
    own_page = pltpu.make_async_copy(
        pagebuf.at[section, own_slot], pagerecv.at[own_slot], page_local
    )
    own_page.start()

    keys = both[:, :HEAD]
    values = both[:, HEAD:]
    scores = lax.dot_general(
        queries, keys, (((1,), (1,)), ((), ())), preferred_element_type=jnp.float32
    ) * (1.0 / HEAD**0.5)
    keep = jnp.concatenate([jnp.where(allowed, 1.0, 0.0)] * heads, axis=0)
    scores = jnp.where(keep > 0.5, scores, -jnp.inf)
    top = jnp.max(scores, axis=1, keepdims=True)
    powers = jnp.exp(scores - top)
    weights = (powers / jnp.sum(powers, axis=1, keepdims=True)).astype(jnp.bfloat16)
    mixed = jnp.dot(weights, values, preferred_element_type=jnp.float32).astype(jnp.bfloat16)
    for h in range(heads):
        attn[:, h * HEAD : (h + 1) * HEAD] = mixed[h * half_rows : (h + 1) * half_rows]

    def sum_copy(n, mask):
        return pltpu.make_async_remote_copy(
            src_ref=joined.at[n, FAR.index(mask)] if mask in FAR else sendbuf.at[n, mate(mask)],
            dst_ref=recvbuf.at[n, mask],
            send_sem=r_send.at[n, mask],
            recv_sem=r_recv.at[n, mask],
            device_id=device(section, mate(1 if mask in HANDED else mask)),
            device_id_type=MESH,
        )

    def join(n):
        for mask in FAR:
            sum_copy(n, mask ^ 1).wait_recv()
            term = held[n, mate(mask)] + recvbuf[n, mask ^ 1].astype(jnp.float32)
            joined[n, FAR.index(mask)] = term.astype(jnp.bfloat16)
            sum_copy(n, mask).start()

    def produce(n, carry):
        out_copy(n).wait()
        partial = jnp.dot(attn[...], wo[n], preferred_element_type=jnp.float32)
        for t in range(tp_count):
            piece = partial[t * rows_dev : (t + 1) * rows_dev]
            held[n, t] = piece
            sendbuf[n, t] = piece.astype(jnp.bfloat16)
        for mask in HANDED + NEAR:
            sum_copy(n, mask).start()

        @pl.when(n >= 1)
        def _():
            join(n - 1)

        return carry

    lax.fori_loop(0, n_chunks, produce, 0)
    join(n_chunks - 1)

    own_page.wait()
    for sec, distance in others:
        page_copy(sec, distance).wait()
    for slot in range(owners):
        pool_ref[0, :, slot * HEAD : (slot + 1) * HEAD] = pagerecv[slot]

    for n in range(n_chunks):
        total = held[n, me]
        for mask in NEAR + FAR:
            sum_copy(n, mask).wait_recv()
            total += recvbuf[n, mask].astype(jnp.float32)
        out_ref[:, n * nc : (n + 1) * nc] = total.astype(jnp.bfloat16)

    for c in range(k_chunks):
        for mask in FAR + NEAR:
            row_copy(c, mask).wait_send()
        for mask in FAR:
            pass_on(c, mask).wait_send()
    for n in range(n_chunks):
        for mask in HANDED + NEAR + FAR:
            sum_copy(n, mask).wait_send()


def fused_body(prompt_rows, query_weight, cache_weight, output_weight, documents, page_table):
    tp_count = lax.axis_size("tp")
    section_count = lax.axis_size("section")
    rows_dev, depth = prompt_rows.shape
    width = query_weight.shape[1]
    out_width = output_weight.shape[1]
    half_rows = rows_dev * tp_count
    owners = section_count * tp_count
    k_chunks = K_CHUNKS
    n_chunks = N_CHUNKS
    kc, nc = depth // k_chunks, out_width // n_chunks
    bf16, f32 = jnp.bfloat16, jnp.float32
    dma = pltpu.SemaphoreType.DMA
    anywhere = pl.BlockSpec(memory_space=pl.ANY)
    local = pl.BlockSpec(memory_space=pltpu.VMEM)
    return pl.pallas_call(
        functools.partial(fused_kernel, (tp_count, section_count, k_chunks, n_chunks)),
        out_shape=(
            jax.ShapeDtypeStruct((rows_dev, out_width), bf16),
            jax.ShapeDtypeStruct((1, PAGE, owners * HEAD), bf16),
        ),
        in_specs=[anywhere] * 4 + [local] * 2,
        out_specs=(local, local),
        scratch_shapes=[
            pltpu.VMEM((k_chunks, tp_count, rows_dev, kc), bf16),
            pltpu.VMEM((k_chunks, kc, width), bf16),
            pltpu.VMEM((k_chunks, kc, 2 * HEAD), bf16),
            pltpu.VMEM((n_chunks, width, nc), bf16),
            pltpu.VMEM((half_rows, width), f32),
            pltpu.VMEM((half_rows, 2 * HEAD), f32),
            pltpu.VMEM((section_count, half_rows, 2 * HEAD), bf16),
            pltpu.VMEM((2, owners, PAGE, HEAD), bf16),
            pltpu.VMEM((owners, PAGE, HEAD), bf16),
            pltpu.VMEM((half_rows, width), bf16),
            pltpu.VMEM((n_chunks, tp_count, rows_dev, nc), bf16),
            pltpu.VMEM((n_chunks, tp_count, rows_dev, nc), bf16),
            pltpu.VMEM((n_chunks, tp_count, rows_dev, nc), f32),
            pltpu.VMEM((n_chunks, 2, rows_dev, nc), bf16),
            dma((k_chunks, tp_count)),
            dma((k_chunks, tp_count)),
            dma((k_chunks,)),
            dma((k_chunks, 2)),
            dma((n_chunks,)),
            dma,
            dma,
            dma((section_count, tp_count)),
            dma((section_count, tp_count)),
            dma,
            dma((n_chunks, tp_count)),
            dma((n_chunks, tp_count)),
        ],
        compiler_params=pltpu.CompilerParams(
            collective_id=0, has_side_effects=True, vmem_limit_bytes=60 * 1024 * 1024
        ),
    )(
        prompt_rows,
        query_weight,
        cache_weight,
        output_weight,
        documents.reshape(1, -1),
        page_table.reshape(1, -1),
    )


def fits(prompt_rows, query_weight, page_table):
    tp_count = lax.axis_size("tp")
    one_copy = tp_count == KV_HEADS
    one_slot = prompt_rows.shape[0] // 4 == 1
    return one_copy and one_slot and lax.axis_size("section") == 2


def choose(prompt_rows, query_weight, cache_weight, output_weight, documents, page_table):
    plan = fused_body if fits(prompt_rows, query_weight, page_table) else body
    return plan(prompt_rows, query_weight, cache_weight, output_weight, documents, page_table)


def solution(mesh):
    return jax.shard_map(
        choose,
        mesh=mesh,
        in_specs=(
            P(("parts", "section", "tp"), None),
            P(None, "tp"),
            P("tp", None, None),
            P("tp", None),
            P("parts"),
            P("parts"),
        ),
        out_specs=(P(("parts", "section", "tp"), None), P(("parts", "section", "tp"), None, None)),
        check_vma=False,
    )
```

```python
import functools
import math

import jax
import jax.numpy as jnp
from jax import lax
from jax.experimental import pallas as pl
from jax.experimental.pallas import tpu as pltpu
from jax.sharding import PartitionSpec as P

KV_HEADS = 8
HEAD = 128
PAGE = 8
K_CHUNKS = 2
N_CHUNKS = 2
MESH = pl.DeviceIdType.MESH
FAR = (4, 6)
NEAR = (1, 2, 3)
HANDED = (5, 7)


rope_base = 500000.0


def from_partner(value, axis, distance):
    mask = 2**distance
    pairs = [(source, source ^ mask) for source in range(lax.axis_size(axis))]
    return lax.ppermute(value, axis, pairs)


def document_layout(documents):
    count = documents.shape[0]
    places = jnp.arange(count, dtype=jnp.int32)
    begins = jnp.concatenate([jnp.ones((1,), dtype=bool), documents[1:] != documents[:-1]])
    firsts = lax.cummax(jnp.where(begins, places, jnp.zeros_like(places)), axis=0)
    offsets = places - firsts
    starts = (offsets % PAGE == 0).astype(jnp.int32)
    pages = jnp.cumsum(starts) - 1
    return (offsets, pages)


def rope_tables(offsets, width):
    half_width = width // 2
    freqs = rope_base ** (-(jnp.arange(half_width, dtype=jnp.float32) * 2.0 / width))
    angles = offsets.astype(jnp.float32)[:, None] * freqs[None, :]
    return (jnp.cos(angles), jnp.sin(angles))


def rotate(values, cosines, sines):
    half_width = values.shape[-1] // 2
    first = values[..., :half_width]
    second = values[..., half_width:]
    return jnp.concatenate(
        [first * cosines - second * sines, second * cosines + first * sines], axis=-1
    )


def finish_cache(keyvals, cosines, sines):
    rotated = rotate(keyvals[:, :HEAD], cosines, sines)
    return jnp.concatenate([rotated, keyvals[:, HEAD:]], axis=1).astype(jnp.bfloat16)


def body(prompt_rows, query_weight, cache_weight, output_weight, documents, page_table):
    tp_count = lax.axis_size("tp")
    owners = lax.axis_size(("section", "tp"))
    section = lax.axis_index("section")
    column = lax.axis_index("tp")
    rows_dev = prompt_rows.shape[0]
    half_rows = rows_dev * tp_count
    total_rows = 2 * half_rows
    query_width = query_weight.shape[1]
    query_heads = query_width // HEAD
    replicas = tp_count // KV_HEADS
    slice_width = HEAD // replicas
    head_weight = cache_weight[0]
    offsets, pages = document_layout(documents)
    cosines, sines = rope_tables(offsets, HEAD)
    own_start = section * half_rows
    own_cos = lax.dynamic_slice_in_dim(cosines, own_start, half_rows, 0)
    own_sin = lax.dynamic_slice_in_dim(sines, own_start, half_rows, 0)
    piece = lax.all_gather(prompt_rows, "tp", axis=0, tiled=True)
    query_rows = jnp.dot(piece, query_weight, preferred_element_type=jnp.float32)
    cache_rows = jnp.dot(piece, head_weight, preferred_element_type=jnp.float32)
    joined = jnp.concatenate([query_rows, cache_rows], axis=1)
    query_part = joined[:, :query_width]
    cache_half = finish_cache(joined[:, query_width:], own_cos, own_sin)
    other = from_partner(cache_half, "section", 0)
    lower = jnp.where(section == 0, cache_half, other)
    upper = jnp.where(section == 0, other, cache_half)
    cache_all = jnp.concatenate([lower, upper], axis=0)
    queries = query_part.reshape(half_rows, query_heads, HEAD)
    queries = rotate(queries, own_cos[:, None, :], own_sin[:, None, :]).astype(jnp.bfloat16)
    keys = cache_all[:, :HEAD]
    values = cache_all[:, HEAD:]
    places = jnp.arange(total_rows, dtype=jnp.int32)
    query_places = own_start + jnp.arange(half_rows, dtype=jnp.int32)
    query_docs = lax.dynamic_slice_in_dim(documents, own_start, half_rows, 0)
    allowed = (query_docs[:, None] == documents[None, :]) & (
        places[None, :] <= query_places[:, None]
    )
    scale = 1.0 / HEAD**0.5
    scores = jnp.einsum("qhd,kd->hqk", queries, keys, preferred_element_type=jnp.float32) * scale
    scores = jnp.where(allowed[None, :, :], scores, -jnp.inf)
    weights = jax.nn.softmax(scores, axis=-1).astype(jnp.bfloat16)
    mixed = jnp.einsum("hqk,kd->qhd", weights, values, preferred_element_type=jnp.float32)
    attention = mixed.astype(jnp.bfloat16).reshape(half_rows, query_heads * HEAD)
    summed = lax.psum_scatter(
        jnp.dot(attention, output_weight, preferred_element_type=jnp.float32),
        "tp",
        scatter_dimension=0,
        tiled=True,
    )
    branch_output = summed.astype(jnp.bfloat16)
    column_start = section * HEAD + column % replicas * slice_width
    share = lax.dynamic_slice_in_dim(cache_all, column_start, slice_width, 1)
    capacity = rows_dev // 4 * PAGE
    row_of = page_table[pages] * PAGE + offsets % PAGE
    outgoing = jnp.zeros((owners * capacity, slice_width), jnp.bfloat16).at[row_of].set(share)
    outgoing = outgoing.reshape(owners, capacity, slice_width)
    arrived = lax.all_to_all(outgoing, ("section", "tp"), split_axis=0, concat_axis=2, tiled=True)
    return (branch_output, arrived)


def fused_kernel(
    sizes,
    rows_hbm,
    wq_hbm,
    wkv_hbm,
    wo_hbm,
    docs_ref,
    table_ref,
    out_ref,
    pool_ref,
    xbuf,
    wq,
    wkv,
    wo,
    acc_q,
    acc_kv,
    kv_all,
    pagebuf,
    pagerecv,
    attn,
    sendbuf,
    recvbuf,
    held,
    joined,
    x_send,
    x_recv,
    x_local,
    w_sem,
    wo_sem,
    kv_send,
    kv_recv,
    page_send,
    page_recv,
    page_local,
    r_send,
    r_recv,
):
    tp_count, section_count, k_chunks, n_chunks = sizes
    part = lax.axis_index("parts")
    section = lax.axis_index("section")
    me = lax.axis_index("tp")
    rows_dev, depth = rows_hbm.shape
    half_rows = rows_dev * tp_count
    total_rows = section_count * half_rows
    kc = depth // k_chunks
    width = wq_hbm.shape[1]
    heads = width // HEAD
    out_width = wo_hbm.shape[1]
    nc = out_width // n_chunks
    owners = section_count * tp_count

    def peer(distance):
        return lax.rem(me + distance, tp_count)

    def mate(mask):
        index = 0
        for bit in (1, 2, 4):
            digit = lax.rem(lax.div(me, bit), 2)
            index = index + bit * (1 - digit if mask & bit else digit)
        return index

    def device(sec, col):
        return (part, sec, col)

    barrier = pltpu.get_barrier_semaphore()
    for sec in range(section_count):
        for distance in range(tp_count):
            if sec == 0 and distance == 0:
                continue
            target = device(lax.rem(section + sec, section_count), peer(distance))
            pl.semaphore_signal(barrier, inc=1, device_id=target, device_id_type=MESH)

    def weight_copies(c):
        where = pl.ds(c * kc, kc)
        return (
            pltpu.make_async_copy(wkv_hbm.at[0, where], wkv.at[c], w_sem.at[c, 0]),
            pltpu.make_async_copy(wq_hbm.at[where], wq.at[c], w_sem.at[c, 1]),
        )

    def out_copy(n):
        return pltpu.make_async_copy(
            wo_hbm.at[:, pl.ds(pl.multiple_of(n * nc, nc), nc)], wo.at[n], wo_sem.at[n]
        )

    def row_copy(c, mask):
        return pltpu.make_async_remote_copy(
            src_ref=rows_hbm.at[:, pl.ds(pl.multiple_of(c * kc, kc), kc)],
            dst_ref=xbuf.at[c, me],
            send_sem=x_send.at[c, mask],
            recv_sem=x_recv.at[c, mask],
            device_id=device(section, mate(mask)),
            device_id_type=MESH,
        )

    def pass_on(c, mask):
        return pltpu.make_async_remote_copy(
            src_ref=xbuf.at[c, mate(mask)],
            dst_ref=xbuf.at[c, mate(mask)],
            send_sem=x_send.at[c, mask ^ 1],
            recv_sem=x_recv.at[c, mask ^ 1],
            device_id=device(section, mate(1)),
            device_id_type=MESH,
        )

    def forward(c):
        for mask in FAR:
            row_copy(c, mask).wait_recv()
            pass_on(c, mask).start()

    def own_rows(c):
        return pltpu.make_async_copy(
            rows_hbm.at[:, pl.ds(pl.multiple_of(c * kc, kc), kc)], xbuf.at[c, me], x_local.at[c]
        )

    for copy in weight_copies(0):
        copy.start()
    for c in range(k_chunks):
        own_rows(c).start()
    pl.semaphore_wait(barrier, owners - 1)
    for c in range(k_chunks):
        for mask in FAR + NEAR:
            row_copy(c, mask).start()
    for c in range(1, k_chunks):
        for copy in weight_copies(c):
            copy.start()
    for n in range(n_chunks):
        out_copy(n).start()

    docs = docs_ref[...].astype(jnp.float32)
    table = table_ref[...].astype(jnp.float32)

    def iota(shape, axis):
        return lax.broadcasted_iota(jnp.int32, shape, axis)

    def layout(count, start):
        row_at = iota((count, total_rows), 0) + start
        col_at = iota((count, total_rows), 1)
        own = jnp.sum(jnp.where(row_at == col_at, docs, 0.0), axis=1, keepdims=True)
        return row_at, col_at, own == docs

    def mod_page(values):
        return values - PAGE * jnp.floor(values * (1.0 / PAGE))

    row_at, col_at, same = layout(half_rows, section * half_rows)
    allowed = same & (col_at <= row_at)
    offset_own = jnp.sum(jnp.where(same & (col_at < row_at), 1.0, 0.0), axis=1, keepdims=True)
    lane = iota((half_rows, HEAD), 1)
    half = HEAD // 2
    second = lane >= half
    freq_at = jnp.where(second, lane - half, lane).astype(jnp.float32)
    freqs = jnp.exp(freq_at * (-2.0 / HEAD * math.log(rope_base)))
    angles = offset_own * freqs
    cosines = jnp.cos(angles)
    sines = jnp.sin(angles)
    sines = jnp.where(second, sines, -sines)

    row_at, col_at, same = layout(total_rows, 0)
    offset_col = jnp.sum(jnp.where(same & (col_at < row_at), 1.0, 0.0), axis=1, keepdims=True)
    offset_row = jnp.sum(jnp.where(same & (row_at < col_at), 1.0, 0.0), axis=0, keepdims=True)
    begins = jnp.where((mod_page(offset_col) == 0.0) & (row_at <= col_at), 1.0, 0.0)
    page_row = jnp.sum(begins, axis=0, keepdims=True) - 1.0
    slot_row = jnp.zeros_like(page_row)
    for p in range(table_ref.shape[1]):
        slot_row += jnp.where(page_row == float(p), table[:, p : p + 1], 0.0)
    place_row = slot_row * PAGE + mod_page(offset_row)
    place_at = iota((owners * PAGE, total_rows), 0).astype(jnp.float32)
    select = jnp.where(place_at == place_row, 1.0, 0.0).astype(jnp.bfloat16)

    def rotate_rows(values):
        return values * cosines + pltpu.roll(values, half, 1) * sines

    acc_q[...] = jnp.zeros_like(acc_q)
    acc_kv[...] = jnp.zeros_like(acc_kv)

    kv_copy = pltpu.make_async_remote_copy(
        src_ref=kv_all.at[section],
        dst_ref=kv_all.at[section],
        send_sem=kv_send,
        recv_sem=kv_recv,
        device_id=device(1 - section, me),
        device_id_type=MESH,
    )

    forward(0)

    def project(c, carry):
        @pl.when(c + 1 < k_chunks)
        def _():
            forward(c + 1)

        own_rows(c).wait()
        for mask in NEAR:
            row_copy(c, mask).wait_recv()
        for mask in FAR:
            pass_on(c, mask).wait_recv()
        pieces = [xbuf[c, t].astype(jnp.float32) for t in range(tp_count)]
        block = jnp.concatenate(pieces, axis=0).astype(jnp.bfloat16)
        copies = weight_copies(c)
        copies[0].wait()
        acc_kv[...] += jnp.dot(block, wkv[c], preferred_element_type=jnp.float32)

        @pl.when(c == k_chunks - 1)
        def _():
            keys_own = rotate_rows(acc_kv[:, :HEAD])
            kv_own = jnp.concatenate([keys_own, acc_kv[:, HEAD:]], axis=1)
            kv_all[section] = kv_own.astype(jnp.bfloat16)
            kv_copy.start()

        copies[1].wait()
        acc_q[...] += jnp.dot(block, wq[c], preferred_element_type=jnp.float32)
        return carry

    lax.fori_loop(0, k_chunks, project, 0)

    queries = jnp.concatenate(
        [rotate_rows(acc_q[:, h * HEAD : (h + 1) * HEAD]) for h in range(heads)], axis=0
    ).astype(jnp.bfloat16)
    kv_copy.wait()
    both = jnp.concatenate([kv_all[0], kv_all[1]], axis=0)

    paged = jnp.dot(select, both, preferred_element_type=jnp.float32).astype(jnp.bfloat16)
    for kind in range(2):
        for q in range(owners):
            pagebuf[kind, q] = paged[q * PAGE : (q + 1) * PAGE, kind * HEAD : (kind + 1) * HEAD]
    own_slot = section * tp_count + me

    def page_copy(sec, distance):
        sec_to = lax.rem(section + sec, section_count)
        to = peer(distance)
        return pltpu.make_async_remote_copy(
            src_ref=pagebuf.at[section, sec_to * tp_count + to],
            dst_ref=pagerecv.at[own_slot],
            send_sem=page_send.at[sec, distance],
            recv_sem=page_recv.at[sec, distance],
            device_id=device(sec_to, to),
            device_id_type=MESH,
        )

    others = [
        (sec, distance)
        for sec in range(section_count)
        for distance in range(tp_count)
        if sec or distance
    ]
    for sec, distance in others:
        page_copy(sec, distance).start()
    own_page = pltpu.make_async_copy(
        pagebuf.at[section, own_slot], pagerecv.at[own_slot], page_local
    )
    own_page.start()

    keys = both[:, :HEAD]
    values = both[:, HEAD:]
    scores = lax.dot_general(
        queries, keys, (((1,), (1,)), ((), ())), preferred_element_type=jnp.float32
    ) * (1.0 / HEAD**0.5)
    keep = jnp.concatenate([jnp.where(allowed, 1.0, 0.0)] * heads, axis=0)
    scores = jnp.where(keep > 0.5, scores, -jnp.inf)
    top = jnp.max(scores, axis=1, keepdims=True)
    powers = jnp.exp(scores - top)
    weights = (powers / jnp.sum(powers, axis=1, keepdims=True)).astype(jnp.bfloat16)
    mixed = jnp.dot(weights, values, preferred_element_type=jnp.float32).astype(jnp.bfloat16)
    for h in range(heads):
        attn[:, h * HEAD : (h + 1) * HEAD] = mixed[h * half_rows : (h + 1) * half_rows]

    def sum_copy(n, mask):
        return pltpu.make_async_remote_copy(
            src_ref=joined.at[n, FAR.index(mask)] if mask in FAR else sendbuf.at[n, mate(mask)],
            dst_ref=recvbuf.at[n, mask],
            send_sem=r_send.at[n, mask],
            recv_sem=r_recv.at[n, mask],
            device_id=device(section, mate(1 if mask in HANDED else mask)),
            device_id_type=MESH,
        )

    def join(n):
        for mask in FAR:
            sum_copy(n, mask ^ 1).wait_recv()
            term = held[n, mate(mask)] + recvbuf[n, mask ^ 1].astype(jnp.float32)
            joined[n, FAR.index(mask)] = term.astype(jnp.bfloat16)
            sum_copy(n, mask).start()

    def produce(n, carry):
        out_copy(n).wait()
        partial = jnp.dot(attn[...], wo[n], preferred_element_type=jnp.float32)
        for t in range(tp_count):
            piece = partial[t * rows_dev : (t + 1) * rows_dev]
            held[n, t] = piece
            sendbuf[n, t] = piece.astype(jnp.bfloat16)
        for mask in HANDED + NEAR:
            sum_copy(n, mask).start()

        @pl.when(n >= 1)
        def _():
            join(n - 1)

        return carry

    lax.fori_loop(0, n_chunks, produce, 0)
    join(n_chunks - 1)

    own_page.wait()
    for sec, distance in others:
        page_copy(sec, distance).wait()
    for slot in range(owners):
        pool_ref[0, :, slot * HEAD : (slot + 1) * HEAD] = pagerecv[slot]

    for n in range(n_chunks):
        total = held[n, me]
        for mask in NEAR + FAR:
            sum_copy(n, mask).wait_recv()
            total += recvbuf[n, mask].astype(jnp.float32)
        out_ref[:, n * nc : (n + 1) * nc] = total.astype(jnp.bfloat16)

    for c in range(k_chunks):
        for mask in FAR + NEAR:
            row_copy(c, mask).wait_send()
        for mask in FAR:
            pass_on(c, mask).wait_send()
    for n in range(n_chunks):
        for mask in HANDED + NEAR + FAR:
            sum_copy(n, mask).wait_send()


def fused_body(prompt_rows, query_weight, cache_weight, output_weight, documents, page_table):
    tp_count = lax.axis_size("tp")
    section_count = lax.axis_size("section")
    rows_dev, depth = prompt_rows.shape
    width = query_weight.shape[1]
    out_width = output_weight.shape[1]
    half_rows = rows_dev * tp_count
    owners = section_count * tp_count
    k_chunks = K_CHUNKS
    n_chunks = N_CHUNKS
    kc, nc = depth // k_chunks, out_width // n_chunks
    bf16, f32 = jnp.bfloat16, jnp.float32
    dma = pltpu.SemaphoreType.DMA
    anywhere = pl.BlockSpec(memory_space=pl.ANY)
    local = pl.BlockSpec(memory_space=pltpu.VMEM)
    summed, pages = pl.pallas_call(
        functools.partial(fused_kernel, (tp_count, section_count, k_chunks, n_chunks)),
        out_shape=(
            jax.ShapeDtypeStruct((rows_dev, out_width), bf16),
            jax.ShapeDtypeStruct((1, PAGE, owners * HEAD), bf16),
        ),
        in_specs=[anywhere] * 4 + [local] * 2,
        out_specs=(local, local),
        scratch_shapes=[
            pltpu.VMEM((k_chunks, tp_count, rows_dev, kc), bf16),
            pltpu.VMEM((k_chunks, kc, width), bf16),
            pltpu.VMEM((k_chunks, kc, 2 * HEAD), bf16),
            pltpu.VMEM((n_chunks, width, nc), bf16),
            pltpu.VMEM((half_rows, width), f32),
            pltpu.VMEM((half_rows, 2 * HEAD), f32),
            pltpu.VMEM((section_count, half_rows, 2 * HEAD), bf16),
            pltpu.VMEM((2, owners, PAGE, HEAD), bf16),
            pltpu.VMEM((owners, PAGE, HEAD), bf16),
            pltpu.VMEM((half_rows, width), bf16),
            pltpu.VMEM((n_chunks, tp_count, rows_dev, nc), bf16),
            pltpu.VMEM((n_chunks, tp_count, rows_dev, nc), bf16),
            pltpu.VMEM((n_chunks, tp_count, rows_dev, nc), f32),
            pltpu.VMEM((n_chunks, 2, rows_dev, nc), bf16),
            dma((k_chunks, tp_count)),
            dma((k_chunks, tp_count)),
            dma((k_chunks,)),
            dma((k_chunks, 2)),
            dma((n_chunks,)),
            dma,
            dma,
            dma((section_count, tp_count)),
            dma((section_count, tp_count)),
            dma,
            dma((n_chunks, tp_count)),
            dma((n_chunks, tp_count)),
        ],
        compiler_params=pltpu.CompilerParams(
            collective_id=0, has_side_effects=True, vmem_limit_bytes=60 * 1024 * 1024
        ),
    )(
        prompt_rows,
        query_weight,
        cache_weight,
        output_weight,
        documents.reshape(1, -1),
        page_table.reshape(1, -1),
    )
    return pl.pallas_call(
        write_kernel,
        out_shape=(
            jax.ShapeDtypeStruct(summed.shape, bf16),
            jax.ShapeDtypeStruct(pages.shape, bf16),
        ),
        in_specs=[local] * 2,
        out_specs=(anywhere, anywhere),
        scratch_shapes=[dma((2,))],
    )(summed, pages)


def write_kernel(summed_ref, pages_ref, out_ref, pool_ref, sems):
    copies = (
        pltpu.make_async_copy(summed_ref, out_ref, sems.at[0]),
        pltpu.make_async_copy(pages_ref, pool_ref, sems.at[1]),
    )
    for copy in copies:
        copy.start()
    for copy in copies:
        copy.wait()


def fits(prompt_rows, query_weight, page_table):
    tp_count = lax.axis_size("tp")
    one_copy = tp_count == KV_HEADS
    one_slot = prompt_rows.shape[0] // 4 == 1
    return one_copy and one_slot and lax.axis_size("section") == 2


def choose(prompt_rows, query_weight, cache_weight, output_weight, documents, page_table):
    plan = fused_body if fits(prompt_rows, query_weight, page_table) else body
    return plan(prompt_rows, query_weight, cache_weight, output_weight, documents, page_table)


def solution(mesh):
    return jax.shard_map(
        choose,
        mesh=mesh,
        in_specs=(
            P(("parts", "section", "tp"), None),
            P(None, "tp"),
            P("tp", None, None),
            P("tp", None),
            P("parts"),
            P("parts"),
        ),
        out_specs=(P(("parts", "section", "tp"), None), P(("parts", "section", "tp"), None, None)),
        check_vma=False,
    )
```
